768 devices in a mesh: ctx: 48 (over z, x), seq: 16 (over y, core).
Axes of the slice: x: 4, y: 8, z: 12, core: 2. Of those that a mesh axis runs over, the one named last changes fastest.
Arguments:
- queries: bfloat16 [24576, 8192], P('ctx', 'seq'), may hold values from -0.375 to 0.375
- keys: bfloat16 [24576, 8192], P('ctx', 'seq'), may hold values from -0.375 to 0.375
- values: bfloat16 [24576, 8192], P('ctx', 'seq'), may hold values from -6 to 6
- out_grad: bfloat16 [24576, 8192], P('ctx', 'seq'), may hold values from -0.375 to 0.375
Outputs:
- attended: bfloat16 [24576, 8192], P('ctx', 'seq')
- query_grad: bfloat16 [24576, 8192], P('ctx', 'seq')
- key_grad: bfloat16 [24576, 8192], P('ctx', 'seq')
- value_grad: bfloat16 [24576, 8192], P('ctx', 'seq')
The draws below stay inside these ranges and needn't reach their ends.
All inputs are finite; a program needn't handle non-finite values.
Results may differ from the reference program's by a relative error of at most 0.0049.
Values sent between devices are 32-bit elements; how exact they have to be, the bound alone decides.
A program may use at most 128 MiB of HBM per device.

```python
import jax
import jax.numpy as jnp
from jax import lax

H = 64
DH = 128
BLOCK = 128
TOKENS = 24576


def level_of(stream_key, extent, shards, low, high):
    def one(dim, blocks):
        heights = jax.random.uniform(jax.random.fold_in(jax.random.fold_in(stream_key, 6), dim), (blocks,), jnp.float32, low / len(shards), high / len(shards))
        return jnp.repeat(jnp.exp(heights), extent[dim] // blocks).reshape((-1,) + (1,) * (len(extent) - dim - 1))

    loudness = one(*shards[0])
    for cut in shards[1:]:
        loudness = loudness * one(*cut)
    return loudness


def gaussian(own_key, extent, scale, limit, pieces=(), dtype=jnp.bfloat16):
    entries = scale * jax.random.normal(own_key, extent, jnp.float32)
    if pieces:
        entries = entries * level_of(own_key, extent, pieces, -0.22, 0.18)
    return jnp.clip(entries, -limit, limit).astype(dtype)


def setup_inputs(seed: int = 0) -> dict:
    key_of = jax.random.split(jax.random.key(seed), 5)
    queries = gaussian(key_of[0], (TOKENS, H * DH), (1.0 / (TOKENS * DH) ** 0.25), 0.375, ((0, 48), (1, 16)))
    keys = gaussian(key_of[1], (TOKENS, H * DH), (1.0 / (TOKENS * DH) ** 0.25), 0.375, ((0, 48), (1, 16)))
    values = gaussian(key_of[2], (TOKENS, H * DH), 1.0, 6.0, ((0, 48), (1, 16)))
    out_grad = gaussian(key_of[3], (TOKENS, H * DH), (1.0 / (TOKENS * DH) ** 0.25), 0.375, ((0, 48), (1, 16)))
    return dict(queries=queries, keys=keys, values=values, out_grad=out_grad)


def block_terms(qb, kb, vb, gb):
    qf = qb.astype(jnp.float32)
    kf = kb.astype(jnp.float32)
    vf = vb.astype(jnp.float32)
    gf = gb.astype(jnp.float32)
    count = qb.shape[0]
    rows = lax.broadcasted_iota(jnp.int32, (count, count), 0)
    cols = lax.broadcasted_iota(jnp.int32, (count, count), 1)
    causal = (cols <= rows)[None]
    attn = jnp.where(causal, jnp.einsum("thi,shi->hts", qf, kf), 0.0).astype(jnp.bfloat16).astype(jnp.float32)
    grads = jnp.where(causal, jnp.einsum("thj,shj->hts", gf, vf), 0.0).astype(jnp.bfloat16).astype(jnp.float32)
    return qf, kf, vf, gf, attn, grads


def reference(queries, keys, values, out_grad):
    blocks = TOKENS // BLOCK
    shape = (blocks, BLOCK, H, DH)
    qs = queries.reshape(shape)
    ks = keys.reshape(shape)
    vs = values.reshape(shape)
    gs = out_grad.reshape(shape)

    def forward(carry, items):
        qb, kb, vb, gb = items
        qf, kf, vf, gf, attn, grads = block_terms(qb, kb, vb, gb)
        prefix_low = carry.astype(jnp.bfloat16).astype(jnp.float32)
        attended = jnp.einsum("hts,shj->thj", attn, vf) + jnp.einsum("thi,hij->thj", qf, prefix_low)
        query_grad = jnp.einsum("hts,shi->thi", grads, kf) + jnp.einsum("thj,hij->thi", gf, prefix_low)
        kv_block = jnp.einsum("thi,thj->hij", kf, vf)
        return carry + kv_block, (attended.astype(jnp.bfloat16), query_grad.astype(jnp.bfloat16))

    def backward(carry, items):
        qb, kb, vb, gb = items
        qf, kf, vf, gf, attn, grads = block_terms(qb, kb, vb, gb)
        suffix_low = carry.astype(jnp.bfloat16).astype(jnp.float32)
        key_grad = jnp.einsum("hts,thi->shi", grads, qf) + jnp.einsum("shj,hij->shi", vf, suffix_low)
        value_grad = jnp.einsum("hts,thj->shj", attn, gf) + jnp.einsum("shi,hij->shj", kf, suffix_low)
        qg_block = jnp.einsum("thi,thj->hij", qf, gf)
        return carry + qg_block, (key_grad.astype(jnp.bfloat16), value_grad.astype(jnp.bfloat16))

    start = jnp.zeros((H, DH, DH), jnp.float32)
    _, (attended, query_grad) = lax.scan(forward, start, (qs, ks, vs, gs))
    _, (key_grad, value_grad) = lax.scan(backward, start, (qs, ks, vs, gs), reverse=True)
    flat = (TOKENS, H * DH)
    return (attended.reshape(flat), query_grad.reshape(flat), key_grad.reshape(flat), value_grad.reshape(flat))
```

```python
import functools

import jax
import jax.numpy as jnp
from jax import lax
from jax.experimental import pallas as pl
from jax.experimental.pallas import tpu as pltpu
from jax.sharding import PartitionSpec as P

DH = 128
BLOCK = 128
X = 4
MESH = pl.DeviceIdType.MESH
F32 = jnp.float32
BF16 = jnp.bfloat16


def dot(a, b, ca, cb):
    return lax.dot_general(a, b, (((ca,), (cb,)), ((), ())), preferred_element_type=F32)


def kernel(
    nz, nb, q_hbm, k_hbm, v_hbm, g_hbm, *refs,
):
    outs = refs[:4]
    (qs, ks, vs, gs, cum, part, xsend, xrecv, tbuf, zrecv, zsend, zpre, xback, before, obuf,
     in_sem, out_sem, xu_s, xu_r, zu_s, zu_r, zd_s, zd_r, xd_s, xd_r) = refs[4:]
    rows = tbuf.shape[1] // nz
    c = lax.axis_index("ctx")
    seq = lax.axis_index("seq")
    z = c // X
    x = c % X

    def xdev(d):
        return (z * X + (x + d) % X, seq)

    def zdev(d):
        return (((z + d) % nz) * X + x, seq)

    zorder = sorted(range(1, nz), key=lambda d: -min(d, nz - d))

    barrier = pltpu.get_barrier_semaphore()
    for d in range(1, X):
        pl.semaphore_signal(barrier, inc=1, device_id=xdev(d), device_id_type=MESH)
    for d in range(1, nz):
        pl.semaphore_signal(barrier, inc=1, device_id=zdev(d), device_id_type=MESH)

    def cols(s):
        return pl.ds(pl.multiple_of(((x + s) % X) * DH, DH), DH)

    slots = (2, 1, 3, 0)
    loads = {}
    for pair in (((k_hbm, ks, 1), (v_hbm, vs, 2)), ((q_hbm, qs, 0), (g_hbm, gs, 3))):
        for s in slots:
            for hbm, buf, i in pair:
                cp = pltpu.make_async_copy(hbm.at[:, cols(s)], buf.at[s], in_sem.at[i, s])
                cp.start()
                loads[i, s] = cp

    for kind in range(2):
        if tbuf.shape[1] > DH:
            lo = DH if kind == 0 else 0
            tbuf[kind, lo:lo + tbuf.shape[1] - DH, :] = jnp.zeros((tbuf.shape[1] - DH, DH), F32)
    base = (0, tbuf.shape[1] - DH)

    def local_state(kind, s):
        a, b = ((ks, vs), (qs, gs))[kind]
        run = jnp.zeros((DH, DH), F32)
        order = range(nb) if kind == 0 else range(nb - 1, -1, -1)
        for blk in order:
            cum[kind, s, blk] = run
            r = pl.ds(blk * BLOCK, BLOCK)
            run = run + dot(a[s, r, :], b[s, r, :], 0, 0)
        return run

    xup = {}
    for kind in range(2):
        for s in slots:
            for i in ((1, 2), (0, 3))[kind]:
                loads[i, s].wait()
            total = local_state(kind, s)
            if s == 0:
                xrecv[kind, x] = total
            else:
                xsend[kind, s] = total
                if kind == 0 and s == slots[0]:
                    pl.semaphore_wait(barrier, X - 1 + nz - 1)
                cp = pltpu.make_async_remote_copy(
                    xsend.at[kind, s], xrecv.at[kind, x], xu_s.at[kind, s], xu_r.at[kind, s],
                    device_id=xdev(s), device_id_type=MESH)
                cp.start()
                xup[kind, s] = cp

    tri = (lax.broadcasted_iota(jnp.int32, (BLOCK, BLOCK), 1)
           <= lax.broadcasted_iota(jnp.int32, (BLOCK, BLOCK), 0))

    def intra(s):
        def one(blk, carry):
            r = pl.ds(pl.multiple_of(blk * BLOCK, BLOCK), BLOCK)
            q, k, v, g = qs[s, r, :], ks[s, r, :], vs[s, r, :], gs[s, r, :]
            attn = jnp.where(tri, dot(q, k, 1, 1), 0.0).astype(BF16)
            grads = jnp.where(tri, dot(g, v, 1, 1), 0.0).astype(BF16)
            part[0, s, r, :] = dot(attn, v, 1, 0)
            part[1, s, r, :] = dot(grads, k, 1, 0)
            part[2, s, r, :] = dot(grads, q, 0, 0)
            part[3, s, r, :] = dot(attn, g, 0, 0)
            return carry

        lax.fori_loop(0, nb, one, 0)

    def wait_xup(kind):
        for d in (1, 3, 2):
            pltpu.make_async_remote_copy(
                xsend.at[kind, d], xrecv.at[kind, (x + X - d) % X], xu_s.at[kind, d], xu_r.at[kind, d],
                device_id=xdev(d), device_id_type=MESH).wait_recv()

    zup, zdn, xdn = {}, {}, {}
    intra(0)
    for kind in range(2):
        wait_xup(kind)
        total = xrecv[kind, 0]
        for i in range(1, X):
            total = total + xrecv[kind, i]
        tbuf[kind, base[kind]:base[kind] + DH, :] = total
        for d in zorder:
            cp = pltpu.make_async_remote_copy(
                tbuf.at[kind, pl.ds(pl.multiple_of(((z + d) % nz) * rows, 8), rows)],
                zrecv.at[kind, z], zu_s.at[kind, d], zu_r.at[kind, d],
                device_id=zdev(d), device_id_type=MESH)
            cp.start()
            zup[kind, d] = cp
        zrecv[kind, z] = tbuf[kind, pl.ds(pl.multiple_of(z * rows, 8), rows), :]

    intra(1)
    for kind in range(2):
        for d in range(1, nz):
            pltpu.make_async_remote_copy(
                tbuf.at[kind, pl.ds(0, rows)], zrecv.at[kind, (z + nz - d) % nz],
                zu_s.at[kind, d], zu_r.at[kind, d],
                device_id=zdev(d), device_id_type=MESH).wait_recv()
        run = jnp.zeros((rows, DH), F32)
        for i in (range(nz) if kind == 0 else range(nz - 1, -1, -1)):
            zsend[kind, i] = run
            run = run + zrecv[kind, i]
        mine = pl.ds(pl.multiple_of(z * rows, 8), rows)
        for d in zorder:
            cp = pltpu.make_async_remote_copy(
                zsend.at[kind, (z + d) % nz], zpre.at[kind, mine], zd_s.at[kind, d], zd_r.at[kind, d],
                device_id=zdev(d), device_id_type=MESH)
            cp.start()
            zdn[kind, d] = cp
        zpre[kind, mine, :] = zsend[kind, z]

    intra(2)
    for kind in range(2):
        for d in range(1, nz):
            pltpu.make_async_remote_copy(
                zsend.at[kind, 0],
                zpre.at[kind, pl.ds(pl.multiple_of(((z + nz - d) % nz) * rows, 8), rows)],
                zd_s.at[kind, d], zd_r.at[kind, d],
                device_id=zdev(d), device_id_type=MESH).wait_recv()
        run = zpre[kind, base[kind]:base[kind] + DH, :]
        for i in (range(X) if kind == 0 else range(X - 1, -1, -1)):
            xback[kind, i] = run
            run = run + xrecv[kind, i]
        for d in (2, 1, 3):
            cp = pltpu.make_async_remote_copy(
                xback.at[kind, (x + d) % X], before.at[kind, X - d], xd_s.at[kind, d], xd_r.at[kind, d],
                device_id=xdev(d), device_id_type=MESH)
            cp.start()
            xdn[kind, d] = cp
        before[kind, 0] = xback[kind, x]

    intra(3)
    stores = []
    for kind in range(2):
        first, second = ((qs, gs), (vs, ks))[kind]
        for s in (0, 1, 3, 2):
            if s:
                d = X - s
                pltpu.make_async_remote_copy(
                    xback.at[kind, d], before.at[kind, s], xd_s.at[kind, d], xd_r.at[kind, d],
                    device_id=xdev(d), device_id_type=MESH).wait_recv()

            def one(blk, carry, kind=kind, s=s):
                r = pl.ds(pl.multiple_of(blk * BLOCK, BLOCK), BLOCK)
                low = (before[kind, s] + cum[kind, s, blk]).astype(BF16)
                if kind == 0:
                    obuf[0, s, r, :] = (part[0, s, r, :] + dot(qs[s, r, :], low, 1, 0)).astype(BF16)
                    obuf[1, s, r, :] = (part[1, s, r, :] + dot(gs[s, r, :], low, 1, 1)).astype(BF16)
                else:
                    obuf[2, s, r, :] = (part[2, s, r, :] + dot(vs[s, r, :], low, 1, 1)).astype(BF16)
                    obuf[3, s, r, :] = (part[3, s, r, :] + dot(ks[s, r, :], low, 1, 0)).astype(BF16)
                return carry

            lax.fori_loop(0, nb, one, 0)
            for o in (2 * kind, 2 * kind + 1):
                cp = pltpu.make_async_copy(obuf.at[o, s], outs[o].at[:, cols(s)], out_sem.at[o, s])
                cp.start()
                stores.append(cp)

    for group in (xup, zup, zdn, xdn):
        for cp in group.values():
            cp.wait_send()
    for cp in stores:
        cp.wait()


def body(nz, queries, keys, values, out_grad):
    count, width = queries.shape
    nb = count // BLOCK
    assert width == X * DH
    rows = -(-(DH // 8) // nz) * 8
    any_spec = pl.BlockSpec(memory_space=pl.ANY)
    vm = pltpu.VMEM
    dma = pltpu.SemaphoreType.DMA
    shape = jax.ShapeDtypeStruct((count, width), BF16)
    return pl.pallas_call(
        functools.partial(kernel, nz, nb),
        out_shape=(shape,) * 4,
        in_specs=[any_spec] * 4,
        out_specs=(any_spec,) * 4,
        scratch_shapes=[
            vm((X, count, DH), BF16),
            vm((X, count, DH), BF16),
            vm((X, count, DH), BF16),
            vm((X, count, DH), BF16),
            vm((2, X, nb, DH, DH), F32),
            vm((4, X, count, DH), F32),
            vm((2, X, DH, DH), F32),
            vm((2, X, DH, DH), F32),
            vm((2, nz * rows, DH), F32),
            vm((2, nz, rows, DH), F32),
            vm((2, nz, rows, DH), F32),
            vm((2, nz * rows, DH), F32),
            vm((2, X, DH, DH), F32),
            vm((2, X, DH, DH), F32),
            vm((4, X, count, DH), BF16),
            dma((4, X)), dma((4, X)),
            dma((2, X)), dma((2, X)),
            dma((2, nz)), dma((2, nz)),
            dma((2, nz)), dma((2, nz)),
            dma((2, X)), dma((2, X)),
        ],
        compiler_params=pltpu.CompilerParams(
            collective_id=0, has_side_effects=True, vmem_limit_bytes=48 * 1024 * 1024),
    )(queries, keys, values, out_grad)


def solution(mesh):
    nz = mesh.shape["ctx"] // X
    spec = P("ctx", "seq")
    return jax.shard_map(
        functools.partial(body, nz), mesh=mesh, in_specs=(spec,) * 4, out_specs=(spec,) * 4, check_vma=False)
```

```python
import functools

import jax
import jax.numpy as jnp
from jax import lax
from jax.experimental import pallas as pl
from jax.experimental.pallas import tpu as pltpu
from jax.sharding import PartitionSpec as P

DH = 128
BLOCK = 128
X = 4
MESH = pl.DeviceIdType.MESH
F32 = jnp.float32
BF16 = jnp.bfloat16


def dot(a, b, ca, cb):
    return lax.dot_general(a, b, (((ca,), (cb,)), ((), ())), preferred_element_type=F32)


def rounds_of(nz):
    known, dists = 1, []
    while known < nz // 2:
        step = min(known, nz // 2 - known)
        dists.append(step)
        known += step
    return dists


def kernel(
    nz, nb, q_hbm, k_hbm, v_hbm, g_hbm, *refs,
):
    outs = refs[:4]
    (qs, ks, vs, gs, cum, part, xsend, xrecv, tbuf, zrecv, zsend, zpre, xback, before,
     in_sem, ring_sem, xu_s, xu_r, zu_s, zu_r, zd_s, zd_r, xd_s, xd_r) = refs[4:]
    rows = tbuf.shape[1] // nz
    c = lax.axis_index("ctx")
    seq = lax.axis_index("seq")
    z = c // X
    x = c % X

    def xdev(d):
        return (z * X + (x + d) % X, seq)

    def zdev(d):
        return (((z + d) % nz) * X + x, seq)

    def both(d):
        return sorted({d, nz - d})

    zorder = sorted(range(1, nz), key=lambda d: -min(d, nz - d))
    rounds = rounds_of(nz)

    loads = {}

    def load(i, hbm, buf):
        cp = pltpu.make_async_copy(hbm, buf, in_sem.at[i])
        cp.start()
        loads[i] = cp

    load(1, k_hbm, ks)
    load(2, v_hbm, vs)
    barrier = pltpu.get_barrier_semaphore()
    for d in (2, 1, 3):
        pl.semaphore_signal(barrier, inc=1, device_id=xdev(d), device_id_type=MESH)
    for d in both(1):
        pl.semaphore_signal(barrier, inc=1, device_id=zdev(d), device_id_type=MESH)
    load(0, q_hbm, qs)
    load(3, g_hbm, gs)

    def ring_signal(i):
        for d in both(rounds[i]):
            pl.semaphore_signal(ring_sem.at[i], inc=1, device_id=zdev(d), device_id_type=MESH)

    def ring_wait(i):
        pl.semaphore_wait(ring_sem.at[i], len(both(rounds[i])))

    def cols(s):
        return pl.ds(pl.multiple_of(((x + s) % X) * DH, DH), DH)

    slots = (2, 1, 3, 0)
    pad = tbuf.shape[1] - DH
    base = (0, pad)
    for kind in range(2):
        if pad:
            lo = DH if kind == 0 else 0
            tbuf[kind, lo:lo + pad, :] = jnp.zeros((pad, DH), F32)

    def local_state(kind, s):
        a, b = ((ks, vs), (qs, gs))[kind]
        run = jnp.zeros((DH, DH), F32)
        for blk in (range(nb) if kind == 0 else range(nb - 1, -1, -1)):
            cum[kind, s, blk] = run
            r = pl.ds(blk * BLOCK, BLOCK)
            run = run + dot(a[r, cols(s)], b[r, cols(s)], 0, 0)
        return run

    for kind in range(2):
        for i in ((1, 2), (0, 3))[kind]:
            loads[i].wait()
        for s in slots:
            total = local_state(kind, s)
            if s == 0:
                xrecv[kind, x] = total
            else:
                xsend[kind, s - 1] = total
                if kind == 0 and s == slots[0]:
                    pl.semaphore_wait(barrier, X - 1 + len(both(1)))
                pltpu.make_async_remote_copy(
                    xsend.at[kind, s - 1], xrecv.at[kind, x], xu_s.at[kind], xu_r.at[kind],
                    device_id=xdev(s), device_id_type=MESH).start()
        if kind == 0 and rounds:
            ring_signal(0)
    for i in range(1, len(rounds)):
        ring_wait(i - 1)
        ring_signal(i)

    tri = (lax.broadcasted_iota(jnp.int32, (BLOCK, BLOCK), 1)
           <= lax.broadcasted_iota(jnp.int32, (BLOCK, BLOCK), 0))

    def intra(s):
        for blk in range(nb):
            r = pl.ds(blk * BLOCK, BLOCK)
            q, k, v, g = qs[r, cols(s)], ks[r, cols(s)], vs[r, cols(s)], gs[r, cols(s)]
            attn = jnp.where(tri, dot(q, k, 1, 1), 0.0).astype(BF16)
            grads = jnp.where(tri, dot(g, v, 1, 1), 0.0).astype(BF16)
            part[0, s, r, :] = dot(attn, v, 1, 0)
            part[1, s, r, :] = dot(grads, k, 1, 0)
            part[2, s, r, :] = dot(grads, q, 0, 0)
            part[3, s, r, :] = dot(attn, g, 0, 0)

    def group(src, dst, send, recv, dev):
        return pltpu.make_async_remote_copy(src, dst, send, recv, device_id=dev, device_id_type=MESH)

    def xup(kind):
        return group(xsend.at[kind], xrecv.at[kind, pl.ds(0, X - 1)], xu_s.at[kind], xu_r.at[kind], xdev(1))

    def zup(kind):
        part_rows = pl.ds(0, nz - 1)
        return group(zsend.at[kind, part_rows], zrecv.at[kind, part_rows], zu_s.at[kind], zu_r.at[kind], zdev(1))

    def zdn(kind):
        part_rows = pl.ds(0, (nz - 1) * rows)
        return group(tbuf.at[kind, part_rows], zpre.at[kind, part_rows], zd_s.at[kind], zd_r.at[kind], zdev(1))

    def xdn(kind):
        return group(xback.at[kind, pl.ds(0, X - 1)], before.at[kind, pl.ds(0, X - 1)], xd_s.at[kind], xd_r.at[kind, 0], xdev(1))

    intra(0)
    for kind in range(2):
        xup(kind).wait_recv()
        total = xrecv[kind, 0]
        for i in range(1, X):
            total = total + xrecv[kind, i]
        tbuf[kind, base[kind]:base[kind] + DH, :] = total
        if kind == 0 and rounds:
            ring_wait(len(rounds) - 1)
        for d in zorder:
            pltpu.make_async_remote_copy(
                tbuf.at[kind, pl.ds(pl.multiple_of(((z + d) % nz) * rows, 8), rows)],
                zrecv.at[kind, z], zu_s.at[kind], zu_r.at[kind],
                device_id=zdev(d), device_id_type=MESH).start()
        zrecv[kind, z] = tbuf[kind, pl.ds(pl.multiple_of(z * rows, 8), rows), :]

    intra(1)
    for kind in range(2):
        zup(kind).wait_recv()
        run = jnp.zeros((rows, DH), F32)
        for i in (range(nz) if kind == 0 else range(nz - 1, -1, -1)):
            zsend[kind, i] = run
            run = run + zrecv[kind, i]
        mine = pl.ds(pl.multiple_of(z * rows, 8), rows)
        for d in zorder:
            pltpu.make_async_remote_copy(
                zsend.at[kind, (z + d) % nz], zpre.at[kind, mine], zd_s.at[kind], zd_r.at[kind],
                device_id=zdev(d), device_id_type=MESH).start()
        zpre[kind, mine, :] = zsend[kind, z]

    intra(2)
    for kind in range(2):
        zdn(kind).wait_recv()
        run = zpre[kind, base[kind]:base[kind] + DH, :]
        for i in (range(X) if kind == 0 else range(X - 1, -1, -1)):
            xback[kind, i] = run
            run = run + xrecv[kind, i]
        for d in (2, 1, 3):
            pltpu.make_async_remote_copy(
                xback.at[kind, (x + d) % X], before.at[kind, X - d], xd_s.at[kind], xd_r.at[kind, d - 1],
                device_id=xdev(d), device_id_type=MESH).start()
        before[kind, 0] = xback[kind, x]

    intra(3)
    for kind in range(2):
        for s in (0, 1, 3, 2):
            if s:
                group(xback.at[kind, 0], before.at[kind, s], xd_s.at[kind], xd_r.at[kind, X - s - 1], xdev(1)).wait_recv()
            for blk in range(nb):
                r = pl.ds(blk * BLOCK, BLOCK)
                low = (before[kind, s] + cum[kind, s, blk]).astype(BF16)
                if kind == 0:
                    first, second = dot(qs[r, cols(s)], low, 1, 0), dot(gs[r, cols(s)], low, 1, 1)
                else:
                    first, second = dot(vs[r, cols(s)], low, 1, 1), dot(ks[r, cols(s)], low, 1, 0)
                outs[2 * kind][r, cols(s)] = (part[2 * kind, s, r, :] + first).astype(BF16)
                outs[2 * kind + 1][r, cols(s)] = (part[2 * kind + 1, s, r, :] + second).astype(BF16)

    for kind in range(2):
        for phase in (xup, zup, zdn, xdn):
            phase(kind).wait_send()


def write_out(*refs):
    sem = refs[8]
    copies = [pltpu.make_async_copy(refs[i], refs[4 + i], sem.at[i]) for i in range(4)]
    for cp in copies:
        cp.start()
    for cp in copies:
        cp.wait()


def body(nz, queries, keys, values, out_grad):
    count, width = queries.shape
    nb = count // BLOCK
    assert width == X * DH
    rows = -(-(DH // 8) // nz) * 8
    hbm = pl.BlockSpec(memory_space=pltpu.HBM)
    vmem = pl.BlockSpec(memory_space=pltpu.VMEM)
    vm = pltpu.VMEM
    dma = pltpu.SemaphoreType.DMA
    shape = jax.ShapeDtypeStruct((count, width), BF16)
    outs = pl.pallas_call(
        functools.partial(kernel, nz, nb),
        out_shape=(pltpu.VMEM((count, width), BF16),) * 4,
        in_specs=[hbm] * 4,
        out_specs=(vmem,) * 4,
        scratch_shapes=[
            vm((count, width), BF16),
            vm((count, width), BF16),
            vm((count, width), BF16),
            vm((count, width), BF16),
            vm((2, X, nb, DH, DH), F32),
            vm((4, X, count, DH), F32),
            vm((2, X - 1, DH, DH), F32),
            vm((2, X, DH, DH), F32),
            vm((2, nz * rows, DH), F32),
            vm((2, nz, rows, DH), F32),
            vm((2, nz, rows, DH), F32),
            vm((2, nz * rows, DH), F32),
            vm((2, X, DH, DH), F32),
            vm((2, X, DH, DH), F32),
            dma((4,)),
            pltpu.SemaphoreType.REGULAR((max(1, len(rounds_of(nz))),)),
            dma((2,)), dma((2,)),
            dma((2,)), dma((2,)),
            dma((2,)), dma((2,)),
            dma((2,)), dma((2, X - 1)),
        ],
        compiler_params=pltpu.CompilerParams(
            collective_id=0, has_side_effects=True, vmem_limit_bytes=32 * 1024 * 1024),
    )(*(pltpu.with_memory_space_constraint(a, pltpu.HBM) for a in (queries, keys, values, out_grad)))
    return pl.pallas_call(
        write_out,
        out_shape=(shape,) * 4,
        in_specs=[vmem] * 4,
        out_specs=(hbm,) * 4,
        scratch_shapes=[dma((4,))],
    )(*(pltpu.with_memory_space_constraint(a, pltpu.VMEM) for a in outs))


def solution(mesh):
    nz = mesh.shape["ctx"] // X
    spec = P("ctx", "seq")
    return jax.shard_map(
        functools.partial(body, nz), mesh=mesh, in_specs=(spec,) * 4, out_specs=(spec,) * 4, check_vma=False)
```

```python
import functools

import jax
import jax.numpy as jnp
from jax import lax
from jax.experimental import pallas as pl
from jax.experimental.pallas import tpu as pltpu
from jax.sharding import PartitionSpec as P

DH = 128
BLOCK = 128
X = 4
HALVES = 2
HALF = DH // HALVES
CHUNKS = tuple((kind, half) for kind in range(2) for half in range(HALVES))
MESH = pl.DeviceIdType.MESH
F32 = jnp.float32
BF16 = jnp.bfloat16


def dot(a, b, ca, cb):
    return lax.dot_general(a, b, (((ca,), (cb,)), ((), ())), preferred_element_type=F32)


def rounds_of(nz):
    known, dists = 1, []
    while known < nz // 2:
        step = min(known, nz // 2 - known)
        dists.append(step)
        known += step
    return dists


def kernel(
    nz, nb, q_hbm, k_hbm, v_hbm, g_hbm, *refs,
):
    outs = refs[:4]
    (qs, ks, vs, gs, cum, part, xsend, xrecv, tbuf, zrecv, zsend, zpre, xback, before,
     in_sem, kv_sem, ring_sem, xu_s, xu_r, zu_s, zu_r, zd_s, zd_r, xd_s, xd_r) = refs[4:]
    owners = 2 * nz // 3
    rows = HALF // owners
    c = lax.axis_index("ctx")
    seq = lax.axis_index("seq")
    z = c // X
    x = c % X

    def xdev(d):
        return (z * X + (x + d) % X, seq)

    def zdev(d):
        return (((z + d) % nz) * X + x, seq)

    def both(d):
        return sorted({d, nz - d})

    def owns(n, at):
        return at % 3 != (2, 0, 1, 2)[n % 4]

    def owned(n, at):
        place = (at % 3, at % 3 - 1, (at % 3) // 2, at % 3)[n % 4]
        return pl.ds(pl.multiple_of((n % HALVES) * HALF + ((at // 3) * 2 + place) * rows, 8), rows)

    def half_rows(half):
        return pl.ds(half * HALF, HALF)

    zorder = sorted(range(1, nz), key=lambda d: -min(d, nz - d))
    rounds = rounds_of(nz)

    def cols(s):
        return pl.ds(pl.multiple_of(((x + s) % X) * DH, DH), DH)

    slots = (2, 1, 3, 0)
    loads = {}

    def load(i, hbm, buf):
        cp = pltpu.make_async_copy(hbm, buf, in_sem.at[i])
        cp.start()
        loads[i] = cp

    for s in slots:
        for i, hbm, buf in ((1, k_hbm, ks), (2, v_hbm, vs)):
            cp = pltpu.make_async_copy(hbm.at[:, cols(s)], buf.at[:, cols(s)], kv_sem.at[i - 1, s])
            cp.start()
            loads[i, s] = cp
    barrier = pltpu.get_barrier_semaphore()
    for d in (2, 1, 3):
        pl.semaphore_signal(barrier, inc=1, device_id=xdev(d), device_id_type=MESH)
    for d in both(1):
        pl.semaphore_signal(barrier, inc=1, device_id=zdev(d), device_id_type=MESH)
    load(0, q_hbm, qs)
    load(3, g_hbm, gs)

    def ring_signal(i):
        for d in both(rounds[i]):
            pl.semaphore_signal(ring_sem.at[i], inc=1, device_id=zdev(d), device_id_type=MESH)

    def ring_wait(i):
        pl.semaphore_wait(ring_sem.at[i], len(both(rounds[i])))

    def local_state(kind, s):
        a, b = ((ks, vs), (qs, gs))[kind]
        run = jnp.zeros((DH, DH), F32)
        for blk in (range(nb) if kind == 0 else range(nb - 1, -1, -1)):
            cum[kind, s, blk] = run
            r = pl.ds(blk * BLOCK, BLOCK)
            run = run + dot(a[r, cols(s)], b[r, cols(s)], 0, 0)
        return run

    def send_state(kind, s, half):
        n = kind * HALVES + half
        pltpu.make_async_remote_copy(
            xsend.at[kind, s - 1, half_rows(half)], xrecv.at[kind, x, half_rows(half)], xu_s.at[n], xu_r.at[n],
            device_id=xdev(s), device_id_type=MESH).start()

    for kind in range(2):
        if kind == 1:
            loads[0].wait()
            loads[3].wait()
        for s in slots:
            if kind == 0:
                loads[1, s].wait()
                loads[2, s].wait()
            total = local_state(kind, s)
            if s == 0:
                xrecv[kind, x] = total
            else:
                xsend[kind, s - 1] = total
                if kind == 0 and s == slots[0]:
                    pl.semaphore_wait(barrier, X - 1 + len(both(1)))
                send_state(kind, s, 0)
        for half in range(1, HALVES):
            for s in slots[:-1]:
                send_state(kind, s, half)
        if kind == 0 and rounds:
            ring_signal(0)
    for i in range(1, len(rounds)):
        ring_wait(i - 1)
        ring_signal(i)

    tri = (lax.broadcasted_iota(jnp.int32, (BLOCK, BLOCK), 1)
           <= lax.broadcasted_iota(jnp.int32, (BLOCK, BLOCK), 0))

    def intra(s):
        for blk in range(nb):
            r = pl.ds(blk * BLOCK, BLOCK)
            q, k, v, g = qs[r, cols(s)], ks[r, cols(s)], vs[r, cols(s)], gs[r, cols(s)]
            attn = jnp.where(tri, dot(q, k, 1, 1), 0.0).astype(BF16)
            grads = jnp.where(tri, dot(g, v, 1, 1), 0.0).astype(BF16)
            part[0, s, r, :] = dot(attn, v, 1, 0)
            part[1, s, r, :] = dot(grads, k, 1, 0)
            part[2, s, r, :] = dot(grads, q, 0, 0)
            part[3, s, r, :] = dot(attn, g, 0, 0)

    def group(src, dst, send, recv, dev):
        return pltpu.make_async_remote_copy(src, dst, send, recv, device_id=dev, device_id_type=MESH)

    def xup(n):
        kind, half = CHUNKS[n]
        return group(xsend.at[kind, pl.ds(0, X - 1), half_rows(half)], xrecv.at[kind, pl.ds(0, X - 1), half_rows(half)],
                     xu_s.at[n], xu_r.at[n], xdev(1))

    def zup(n, count):
        return group(zsend.at[n, pl.ds(0, count)], zrecv.at[n, pl.ds(0, count)], zu_s.at[n], zu_r.at[n], zdev(1))

    def zdn(n, count):
        return group(zsend.at[n, pl.ds(0, count)], zrecv.at[n, pl.ds(0, count)], zd_s.at[n], zd_r.at[n], zdev(1))

    def xdn(n, count, d):
        kind, half = CHUNKS[n]
        return group(xback.at[kind, pl.ds(0, count), half_rows(half)], before.at[kind, pl.ds(0, count), half_rows(half)],
                     xd_s.at[n], xd_r.at[n, d - 1], xdev(1))

    intra(0)
    for n, (kind, half) in enumerate(CHUNKS):
        xup(n).wait_recv()
        total = xrecv[kind, 0, half_rows(half), :]
        for i in range(1, X):
            total = total + xrecv[kind, i, half_rows(half), :]
        tbuf[kind, half_rows(half), :] = total
        if n == 0 and rounds:
            ring_wait(len(rounds) - 1)
        for d in zorder:
            to = (z + d) % nz

            @pl.when(owns(n, to))
            def _(n=n, kind=kind, d=d, to=to):
                pltpu.make_async_remote_copy(
                    tbuf.at[kind, owned(n, to)], zrecv.at[n, z], zu_s.at[n], zu_r.at[n],
                    device_id=zdev(d), device_id_type=MESH).start()

    intra(1)
    for n, (kind, half) in enumerate(CHUNKS):

        @pl.when(owns(n, z))
        def _(n=n, kind=kind):
            mine = owned(n, z)
            zrecv[n, z] = tbuf[kind, mine, :]
            zup(n, nz - 1).wait_recv()
            run = jnp.zeros((rows, DH), F32)
            for i in (range(nz) if kind == 0 else range(nz - 1, -1, -1)):
                zsend[n, i] = run
                run = run + zrecv[n, i]
            for d in zorder:
                pltpu.make_async_remote_copy(
                    zsend.at[n, (z + d) % nz], zpre.at[kind, mine], zd_s.at[n], zd_r.at[n],
                    device_id=zdev(d), device_id_type=MESH).start()
            zpre[kind, mine, :] = zsend[n, z]

    intra(2)
    for n, (kind, half) in enumerate(CHUNKS):
        @pl.when(owns(n, z))
        def _(n=n):
            zdn(n, owners - 1).wait_recv()

        @pl.when(jnp.logical_not(owns(n, z)))
        def _(n=n):
            zdn(n, owners).wait_recv()

        run = zpre[kind, half_rows(half), :]
        for i in (range(X) if kind == 0 else range(X - 1, -1, -1)):
            xback[kind, i, half_rows(half), :] = run
            run = run + xrecv[kind, i, half_rows(half), :]
        for d in (2, 1, 3):
            pltpu.make_async_remote_copy(
                xback.at[kind, (x + d) % X, half_rows(half)], before.at[kind, X - d, half_rows(half)],
                xd_s.at[n], xd_r.at[n, d - 1], device_id=xdev(d), device_id_type=MESH).start()
        before[kind, 0, half_rows(half), :] = xback[kind, x, half_rows(half), :]

    intra(3)
    for kind in range(2):
        for s in (0, 1, 3, 2):
            if s:
                for half in range(HALVES):
                    xdn(kind * HALVES + half, 1, X - s).wait_recv()
            for blk in range(nb):
                r = pl.ds(blk * BLOCK, BLOCK)
                low = (before[kind, s] + cum[kind, s, blk]).astype(BF16)
                if kind == 0:
                    first, second = dot(qs[r, cols(s)], low, 1, 0), dot(gs[r, cols(s)], low, 1, 1)
                else:
                    first, second = dot(vs[r, cols(s)], low, 1, 1), dot(ks[r, cols(s)], low, 1, 0)
                outs[2 * kind][r, cols(s)] = (part[2 * kind, s, r, :] + first).astype(BF16)
                outs[2 * kind + 1][r, cols(s)] = (part[2 * kind + 1, s, r, :] + second).astype(BF16)

    for n in range(len(CHUNKS)):
        xup(n).wait_send()

        @pl.when(owns(n, z))
        def _(n=n):
            zup(n, owners - 1).wait_send()
            zdn(n, nz - 1).wait_send()

        @pl.when(jnp.logical_not(owns(n, z)))
        def _(n=n):
            zup(n, owners).wait_send()

        xdn(n, X - 1, 1).wait_send()


def write_out(*refs):
    sem = refs[8]
    copies = [pltpu.make_async_copy(refs[i], refs[4 + i], sem.at[i]) for i in range(4)]
    for cp in copies:
        cp.start()
    for cp in copies:
        cp.wait()


def body(nz, queries, keys, values, out_grad):
    count, width = queries.shape
    nb = count // BLOCK
    assert width == X * DH
    assert nz % 3 == 0 and HALF * 3 % (2 * nz) == 0
    rows = HALF * 3 // (2 * nz)
    nc = len(CHUNKS)
    hbm = pl.BlockSpec(memory_space=pltpu.HBM)
    vmem = pl.BlockSpec(memory_space=pltpu.VMEM)
    vm = pltpu.VMEM
    dma = pltpu.SemaphoreType.DMA
    shape = jax.ShapeDtypeStruct((count, width), BF16)
    outs = pl.pallas_call(
        functools.partial(kernel, nz, nb),
        out_shape=(pltpu.VMEM((count, width), BF16),) * 4,
        in_specs=[hbm] * 4,
        out_specs=(vmem,) * 4,
        scratch_shapes=[
            vm((count, width), BF16),
            vm((count, width), BF16),
            vm((count, width), BF16),
            vm((count, width), BF16),
            vm((2, X, nb, DH, DH), F32),
            vm((4, X, count, DH), F32),
            vm((2, X - 1, DH, DH), F32),
            vm((2, X, DH, DH), F32),
            vm((2, DH, DH), F32),
            vm((nc, nz, rows, DH), F32),
            vm((nc, nz, rows, DH), F32),
            vm((2, DH, DH), F32),
            vm((2, X, DH, DH), F32),
            vm((2, X, DH, DH), F32),
            dma((4,)), dma((2, X)),
            pltpu.SemaphoreType.REGULAR((max(1, len(rounds_of(nz))),)),
            dma((nc,)), dma((nc,)),
            dma((nc,)), dma((nc,)),
            dma((nc,)), dma((nc,)),
            dma((nc,)), dma((nc, X - 1)),
        ],
        compiler_params=pltpu.CompilerParams(
            collective_id=0, has_side_effects=True, vmem_limit_bytes=32 * 1024 * 1024),
    )(*(pltpu.with_memory_space_constraint(a, pltpu.HBM) for a in (queries, keys, values, out_grad)))
    return pl.pallas_call(
        write_out,
        out_shape=(shape,) * 4,
        in_specs=[vmem] * 4,
        out_specs=(hbm,) * 4,
        scratch_shapes=[dma((4,))],
    )(*(pltpu.with_memory_space_constraint(a, pltpu.VMEM) for a in outs))


def solution(mesh):
    nz = mesh.shape["ctx"] // X
    spec = P("ctx", "seq")
    return jax.shard_map(
        functools.partial(body, nz), mesh=mesh, in_specs=(spec,) * 4, out_specs=(spec,) * 4, check_vma=False)
```

```python
import functools

import jax
import jax.numpy as jnp
from jax import lax
from jax.experimental import pallas as pl
from jax.experimental.pallas import tpu as pltpu
from jax.sharding import PartitionSpec as P

DH = 128
BLOCK = 128
X = 4
HALVES = 2
HALF = DH // HALVES
CHUNKS = tuple((kind, half) for kind in range(2) for half in range(HALVES))
LATE_FIRST = tuple(sorted(range(len(CHUNKS)), key=lambda n: -CHUNKS[n][0]))
MESH = pl.DeviceIdType.MESH
F32 = jnp.float32
BF16 = jnp.bfloat16


def dot(a, b, ca, cb):
    return lax.dot_general(a, b, (((ca,), (cb,)), ((), ())), preferred_element_type=F32)


def rounds_of(nz):
    known, dists = 1, []
    while known < nz // 2:
        step = min(known, nz // 2 - known)
        dists.append(step)
        known += step
    return dists


def kernel(
    nz, nb, q_hbm, k_hbm, v_hbm, g_hbm, *refs,
):
    outs = refs[:4]
    (qs, ks, vs, gs, cum, part, xsend, xrecv, tbuf, zrecv, zsend, zpre, xback, before,
     in_sem, qg_sem, ring_sem, xu_s, xu_r, zu_s, zu_r, zk_r, zd_s, zd_r, xd_s, xd_r) = refs[4:]
    owners = 2 * nz // 3
    early = nz // 3
    rows = HALF // owners
    c = lax.axis_index("ctx")
    seq = lax.axis_index("seq")
    z = c // X
    x = c % X

    def xdev(d):
        return (z * X + (x + d) % X, seq)

    def zdev(d):
        return (((z + d) % nz) * X + x, seq)

    def both(d):
        return sorted({d, nz - d})

    def owns(n, at):
        return at % 3 != (2, 0, 1, 2)[n % 4]

    def owned(n, at):
        place = (at % 3, at % 3 - 1, (at % 3) // 2, at % 3)[n % 4]
        return pl.ds(pl.multiple_of((n % HALVES) * HALF + ((at // 3) * 2 + place) * rows, 8), rows)

    def arrival(n):
        return zk_r.at[n, jnp.minimum(z, early)] if CHUNKS[n][0] == 0 else zu_r.at[n]

    def half_rows(half):
        return pl.ds(half * HALF, HALF)

    zorder = sorted(range(1, nz), key=lambda d: -min(d, nz - d))
    rounds = rounds_of(nz)

    def cols(s):
        return pl.ds(pl.multiple_of(((x + s) % X) * DH, DH), DH)

    slots = (2, 1, 3, 0)
    loads = {}

    def load(i, hbm, buf):
        cp = pltpu.make_async_copy(hbm, buf, in_sem.at[i])
        cp.start()
        loads[i] = cp

    for s in slots:
        for i, hbm, buf in ((0, q_hbm, qs), (1, g_hbm, gs)):
            cp = pltpu.make_async_copy(hbm.at[:, cols(s)], buf.at[:, cols(s)], qg_sem.at[i, s])
            cp.start()
            loads[i, s] = cp
    barrier = pltpu.get_barrier_semaphore()
    for d in (2, 1, 3):
        pl.semaphore_signal(barrier, inc=1, device_id=xdev(d), device_id_type=MESH)
    for d in both(1):
        pl.semaphore_signal(barrier, inc=1, device_id=zdev(d), device_id_type=MESH)
    load(0, k_hbm, ks)
    load(1, v_hbm, vs)

    def ring_signal(i):
        for d in both(rounds[i]):
            pl.semaphore_signal(ring_sem.at[i], inc=1, device_id=zdev(d), device_id_type=MESH)

    def ring_wait(i):
        pl.semaphore_wait(ring_sem.at[i], len(both(rounds[i])))

    def local_state(kind, s):
        a, b = ((ks, vs), (qs, gs))[kind]
        run = jnp.zeros((DH, DH), F32)
        for blk in (range(nb) if kind == 0 else range(nb - 1, -1, -1)):
            cum[kind, s, blk] = run
            r = pl.ds(blk * BLOCK, BLOCK)
            run = run + dot(a[r, cols(s)], b[r, cols(s)], 0, 0)
        return run

    def send_state(kind, s, half):
        n = kind * HALVES + half
        pltpu.make_async_remote_copy(
            xsend.at[kind, s - 1, half_rows(half)], xrecv.at[kind, x, half_rows(half)], xu_s.at[n], xu_r.at[n],
            device_id=xdev(s), device_id_type=MESH).start()

    for kind in (1, 0):
        if kind == 0:
            loads[0].wait()
            loads[1].wait()
        for s in slots:
            if kind == 1:
                loads[0, s].wait()
                loads[1, s].wait()
            total = local_state(kind, s)
            if s == 0:
                xrecv[kind, x] = total
            else:
                xsend[kind, s - 1] = total
                if kind == 1 and s == slots[0]:
                    pl.semaphore_wait(barrier, X - 1 + len(both(1)))
                send_state(kind, s, 0)
        for half in range(1, HALVES):
            for s in slots[:-1]:
                send_state(kind, s, half)
        if kind == 1 and rounds:
            ring_signal(0)
    for i in range(1, len(rounds)):
        ring_wait(i - 1)
        ring_signal(i)

    tri = (lax.broadcasted_iota(jnp.int32, (BLOCK, BLOCK), 1)
           <= lax.broadcasted_iota(jnp.int32, (BLOCK, BLOCK), 0))

    def intra(s):
        for blk in range(nb):
            r = pl.ds(blk * BLOCK, BLOCK)
            q, k, v, g = qs[r, cols(s)], ks[r, cols(s)], vs[r, cols(s)], gs[r, cols(s)]
            attn = jnp.where(tri, dot(q, k, 1, 1), 0.0).astype(BF16)
            grads = jnp.where(tri, dot(g, v, 1, 1), 0.0).astype(BF16)
            part[0, s, r, :] = dot(attn, v, 1, 0)
            part[1, s, r, :] = dot(grads, k, 1, 0)
            part[2, s, r, :] = dot(grads, q, 0, 0)
            part[3, s, r, :] = dot(attn, g, 0, 0)

    def group(src, dst, send, recv, dev):
        return pltpu.make_async_remote_copy(src, dst, send, recv, device_id=dev, device_id_type=MESH)

    def xup(n):
        kind, half = CHUNKS[n]
        return group(xsend.at[kind, pl.ds(0, X - 1), half_rows(half)], xrecv.at[kind, pl.ds(0, X - 1), half_rows(half)],
                     xu_s.at[n], xu_r.at[n], xdev(1))

    def zup(n, count):
        return group(zsend.at[n, pl.ds(0, count)], zrecv.at[n, pl.ds(0, count)], zu_s.at[n], zu_r.at[n], zdev(1))

    def zdn(n, count):
        return group(zsend.at[n, pl.ds(0, count)], zrecv.at[n, pl.ds(0, count)], zd_s.at[n], zd_r.at[n], zdev(1))

    def xdn(n, count, d):
        kind, half = CHUNKS[n]
        return group(xback.at[kind, pl.ds(0, count), half_rows(half)], before.at[kind, pl.ds(0, count), half_rows(half)],
                     xd_s.at[n], xd_r.at[n, d - 1], xdev(1))

    intra(0)
    for n in LATE_FIRST:
        kind, half = CHUNKS[n]
        xup(n).wait_recv()
        total = xrecv[kind, 0, half_rows(half), :]
        for i in range(1, X):
            total = total + xrecv[kind, i, half_rows(half), :]
        tbuf[kind, half_rows(half), :] = total
        if n == LATE_FIRST[0] and rounds:
            ring_wait(len(rounds) - 1)
        for d in zorder:
            to = (z + d) % nz

            @pl.when(owns(n, to))
            def _(n=n, kind=kind, d=d, to=to):
                pltpu.make_async_remote_copy(
                    tbuf.at[kind, owned(n, to)], zrecv.at[n, z], zu_s.at[n], arrival(n),
                    device_id=zdev(d), device_id_type=MESH).start()

    def give(n, to):
        kind = CHUNKS[n][0]

        @pl.when(z != to)
        def _():
            pltpu.make_async_remote_copy(
                zsend.at[n, to], zpre.at[kind, owned(n, z)], zd_s.at[n], zd_r.at[n],
                device_id=(to * X + x, seq), device_id_type=MESH).start()

        @pl.when(z == to)
        def _():
            zpre[kind, owned(n, z), :] = zsend[n, to]

    def arrived(n, sem, count):
        group(zsend.at[n, pl.ds(0, count)], zrecv.at[n, pl.ds(0, count)], zd_s.at[n], sem, zdev(1)).wait_recv()

    def scan_early(n):
        zrecv[n, z] = tbuf[0, owned(n, z), :]
        run = jnp.zeros((rows, DH), F32)
        for i in range(early + 1):
            zsend[n, i] = run
            give(n, i)
            if i < early:
                @pl.when(z != i)
                def _(i=i):
                    arrived(n, zk_r.at[n, i], 1)

                run = run + zrecv[n, i]

    def scan_late(n):
        @pl.when(z < early)
        def _():
            arrived(n, zk_r.at[n, early], nz - early)

        @pl.when(z >= early)
        def _():
            arrived(n, zk_r.at[n, early], nz - early - 1)

        run = zsend[n, early]
        for i in range(early, nz - 1):
            run = run + zrecv[n, i]
            zsend[n, i + 1] = run
        for i in range(early + 1, nz):
            give(n, i)

    def scan_back(n):
        zrecv[n, z] = tbuf[1, owned(n, z), :]
        arrived(n, zu_r.at[n], nz - 1)
        run = jnp.zeros((rows, DH), F32)
        for i in range(nz - 1, -1, -1):
            zsend[n, i] = run
            run = run + zrecv[n, i]
        for i in range(nz):
            give(n, i)

    intra(1)
    for scan, kind in ((scan_early, 0), (scan_back, 1), (scan_late, 0)):
        for half in range(HALVES):
            n = kind * HALVES + half

            @pl.when(owns(n, z))
            def _(scan=scan, n=n):
                scan(n)

    intra(2)
    for n, (kind, half) in enumerate(CHUNKS):
        @pl.when(owns(n, z))
        def _(n=n):
            zdn(n, owners - 1).wait_recv()

        @pl.when(jnp.logical_not(owns(n, z)))
        def _(n=n):
            zdn(n, owners).wait_recv()

        run = zpre[kind, half_rows(half), :]
        for i in (range(X) if kind == 0 else range(X - 1, -1, -1)):
            xback[kind, i, half_rows(half), :] = run
            run = run + xrecv[kind, i, half_rows(half), :]
        for d in (2, 1, 3):
            pltpu.make_async_remote_copy(
                xback.at[kind, (x + d) % X, half_rows(half)], before.at[kind, X - d, half_rows(half)],
                xd_s.at[n], xd_r.at[n, d - 1], device_id=xdev(d), device_id_type=MESH).start()
        before[kind, 0, half_rows(half), :] = xback[kind, x, half_rows(half), :]

    intra(3)
    for kind in range(2):
        for s in (0, 1, 3, 2):
            if s:
                for half in range(HALVES):
                    xdn(kind * HALVES + half, 1, X - s).wait_recv()
            for blk in range(nb):
                r = pl.ds(blk * BLOCK, BLOCK)
                low = (before[kind, s] + cum[kind, s, blk]).astype(BF16)
                if kind == 0:
                    first, second = dot(qs[r, cols(s)], low, 1, 0), dot(gs[r, cols(s)], low, 1, 1)
                else:
                    first, second = dot(vs[r, cols(s)], low, 1, 1), dot(ks[r, cols(s)], low, 1, 0)
                outs[2 * kind][r, cols(s)] = (part[2 * kind, s, r, :] + first).astype(BF16)
                outs[2 * kind + 1][r, cols(s)] = (part[2 * kind + 1, s, r, :] + second).astype(BF16)

    for n in range(len(CHUNKS)):
        xup(n).wait_send()

        @pl.when(owns(n, z))
        def _(n=n):
            zup(n, owners - 1).wait_send()
            zdn(n, nz - 1).wait_send()

        @pl.when(jnp.logical_not(owns(n, z)))
        def _(n=n):
            zup(n, owners).wait_send()

        xdn(n, X - 1, 1).wait_send()


def write_out(*refs):
    sem = refs[8]
    copies = [pltpu.make_async_copy(refs[i], refs[4 + i], sem.at[i]) for i in range(4)]
    for cp in copies:
        cp.start()
    for cp in copies:
        cp.wait()


def body(nz, queries, keys, values, out_grad):
    count, width = queries.shape
    nb = count // BLOCK
    assert width == X * DH
    assert nz % 3 == 0 and HALF * 3 % (2 * nz) == 0
    rows = HALF * 3 // (2 * nz)
    nc = len(CHUNKS)
    hbm = pl.BlockSpec(memory_space=pltpu.HBM)
    vmem = pl.BlockSpec(memory_space=pltpu.VMEM)
    vm = pltpu.VMEM
    dma = pltpu.SemaphoreType.DMA
    shape = jax.ShapeDtypeStruct((count, width), BF16)
    outs = pl.pallas_call(
        functools.partial(kernel, nz, nb),
        out_shape=(pltpu.VMEM((count, width), BF16),) * 4,
        in_specs=[hbm] * 4,
        out_specs=(vmem,) * 4,
        scratch_shapes=[
            vm((count, width), BF16),
            vm((count, width), BF16),
            vm((count, width), BF16),
            vm((count, width), BF16),
            vm((2, X, nb, DH, DH), F32),
            vm((4, X, count, DH), F32),
            vm((2, X - 1, DH, DH), F32),
            vm((2, X, DH, DH), F32),
            vm((2, DH, DH), F32),
            vm((nc, nz, rows, DH), F32),
            vm((nc, nz, rows, DH), F32),
            vm((2, DH, DH), F32),
            vm((2, X, DH, DH), F32),
            vm((2, X, DH, DH), F32),
            dma((2,)), dma((2, X)),
            pltpu.SemaphoreType.REGULAR((max(1, len(rounds_of(nz))),)),
            dma((nc,)), dma((nc,)),
            dma((nc,)), dma((nc,)), dma((HALVES, nz // 3 + 1)),
            dma((nc,)), dma((nc,)),
            dma((nc,)), dma((nc, X - 1)),
        ],
        compiler_params=pltpu.CompilerParams(
            collective_id=0, has_side_effects=True, vmem_limit_bytes=32 * 1024 * 1024),
    )(*(pltpu.with_memory_space_constraint(a, pltpu.HBM) for a in (queries, keys, values, out_grad)))
    return pl.pallas_call(
        write_out,
        out_shape=(shape,) * 4,
        in_specs=[vmem] * 4,
        out_specs=(hbm,) * 4,
        scratch_shapes=[dma((4,))],
    )(*(pltpu.with_memory_space_constraint(a, pltpu.VMEM) for a in outs))


def solution(mesh):
    nz = mesh.shape["ctx"] // X
    spec = P("ctx", "seq")
    return jax.shard_map(
        functools.partial(body, nz), mesh=mesh, in_specs=(spec,) * 4, out_specs=(spec,) * 4, check_vma=False)
```

```python
import functools

import jax
import jax.numpy as jnp
from jax import lax
from jax.experimental import pallas as pl
from jax.experimental.pallas import tpu as pltpu
from jax.sharding import PartitionSpec as P

DH = 128
BLOCK = 128
X = 4
HALVES = 2
NEAR = 2
HALF = DH // HALVES
CHUNKS = tuple((kind, half) for kind in range(2) for half in range(HALVES))
LATE_FIRST = tuple(sorted(range(len(CHUNKS)), key=lambda n: -CHUNKS[n][0]))
MESH = pl.DeviceIdType.MESH
F32 = jnp.float32
BF16 = jnp.bfloat16


def dot(a, b, ca, cb):
    return lax.dot_general(a, b, (((ca,), (cb,)), ((), ())), preferred_element_type=F32)


def rounds_of(nz):
    known, dists = min(NEAR, nz // 2), []
    while known < nz // 2:
        step = min(known, nz // 2 - known)
        dists.append(step)
        known += step
    return dists


def kernel(
    nz, nb, q_hbm, k_hbm, v_hbm, g_hbm, *refs,
):
    outs = refs[:4]
    (qs, ks, vs, gs, cum, part, xsend, xrecv, tbuf, zrecv, zsend, zpre, xback, before,
     in_sem, qg_sem, ring_sem, xu_s, xu_r, zu_s, zu_r, zk_r, zd_s, zd_r, xd_s, xd_r) = refs[4:]
    owners = 2 * nz // 3
    early = nz // 3
    rows = HALF // owners
    c = lax.axis_index("ctx")
    seq = lax.axis_index("seq")
    z = c // X
    x = c % X

    def xdev(d):
        return (z * X + (x + d) % X, seq)

    def zdev(d):
        return (((z + d) % nz) * X + x, seq)

    def both(d):
        return sorted({d, nz - d})

    def owns(n, at):
        return at % 3 != (2, 0, 1, 2)[n % 4]

    def owned(n, at):
        place = (at % 3, at % 3 - 1, (at % 3) // 2, at % 3)[n % 4]
        return pl.ds(pl.multiple_of((n % HALVES) * HALF + ((at // 3) * 2 + place) * rows, 8), rows)

    def arrival(n):
        return zk_r.at[n, jnp.minimum(z, early)] if CHUNKS[n][0] == 0 else zu_r.at[n]

    def half_rows(half):
        return pl.ds(half * HALF, HALF)

    near = sorted({e for d in range(1, min(NEAR, nz // 2) + 1) for e in both(d)})
    zorder = sorted(range(1, nz), key=lambda d: -min(d, nz - d))
    rounds = rounds_of(nz)

    def cols(s):
        return pl.ds(pl.multiple_of(((x + s) % X) * DH, DH), DH)

    slots = (2, 1, 3, 0)
    loads = {}

    def load(i, hbm, buf):
        cp = pltpu.make_async_copy(hbm, buf, in_sem.at[i])
        cp.start()
        loads[i] = cp

    for s in slots:
        for i, hbm, buf in ((0, q_hbm, qs), (1, g_hbm, gs)):
            cp = pltpu.make_async_copy(hbm.at[:, cols(s)], buf.at[:, cols(s)], qg_sem.at[i, s])
            cp.start()
            loads[i, s] = cp
    barrier = pltpu.get_barrier_semaphore()
    for d in (2, 1, 3):
        pl.semaphore_signal(barrier, inc=1, device_id=xdev(d), device_id_type=MESH)
    for d in near:
        pl.semaphore_signal(barrier, inc=1, device_id=zdev(d), device_id_type=MESH)
    load(0, k_hbm, ks)
    load(1, v_hbm, vs)

    def ring_signal(i):
        for d in both(rounds[i]):
            pl.semaphore_signal(ring_sem.at[i], inc=1, device_id=zdev(d), device_id_type=MESH)

    def ring_wait(i):
        pl.semaphore_wait(ring_sem.at[i], len(both(rounds[i])))

    def local_state(kind, s):
        a, b = ((ks, vs), (qs, gs))[kind]
        run = jnp.zeros((DH, DH), F32)
        for blk in (range(nb) if kind == 0 else range(nb - 1, -1, -1)):
            cum[kind, s, blk] = run
            r = pl.ds(blk * BLOCK, BLOCK)
            run = run + dot(a[r, cols(s)], b[r, cols(s)], 0, 0)
        return run

    def send_state(kind, s, half):
        n = kind * HALVES + half
        pltpu.make_async_remote_copy(
            xsend.at[kind, s - 1, half_rows(half)], xrecv.at[kind, x, half_rows(half)], xu_s.at[n], xu_r.at[n],
            device_id=xdev(s), device_id_type=MESH).start()

    for kind in (1, 0):
        if kind == 0:
            loads[0].wait()
            loads[1].wait()
        for s in slots:
            if kind == 1:
                loads[0, s].wait()
                loads[1, s].wait()
            total = local_state(kind, s)
            if s == 0:
                xrecv[kind, x] = total
            else:
                xsend[kind, s - 1] = total
                if kind == 1 and s == slots[0]:
                    pl.semaphore_wait(barrier, X - 1 + len(near))
                    if rounds:
                        ring_signal(0)
                send_state(kind, s, 0)
        for half in range(1, HALVES):
            for s in slots[:-1]:
                send_state(kind, s, half)
    for i in range(1, len(rounds)):
        ring_wait(i - 1)
        ring_signal(i)

    tri = (lax.broadcasted_iota(jnp.int32, (BLOCK, BLOCK), 1)
           <= lax.broadcasted_iota(jnp.int32, (BLOCK, BLOCK), 0))

    def intra(s):
        for blk in range(nb):
            r = pl.ds(blk * BLOCK, BLOCK)
            q, k, v, g = qs[r, cols(s)], ks[r, cols(s)], vs[r, cols(s)], gs[r, cols(s)]
            attn = jnp.where(tri, dot(q, k, 1, 1), 0.0).astype(BF16)
            grads = jnp.where(tri, dot(g, v, 1, 1), 0.0).astype(BF16)
            part[0, s, r, :] = dot(attn, v, 1, 0)
            part[1, s, r, :] = dot(grads, k, 1, 0)
            part[2, s, r, :] = dot(grads, q, 0, 0)
            part[3, s, r, :] = dot(attn, g, 0, 0)

    def group(src, dst, send, recv, dev):
        return pltpu.make_async_remote_copy(src, dst, send, recv, device_id=dev, device_id_type=MESH)

    def xup(n):
        kind, half = CHUNKS[n]
        return group(xsend.at[kind, pl.ds(0, X - 1), half_rows(half)], xrecv.at[kind, pl.ds(0, X - 1), half_rows(half)],
                     xu_s.at[n], xu_r.at[n], xdev(1))

    def zup(n, count):
        return group(zsend.at[n, pl.ds(0, count)], zrecv.at[n, pl.ds(0, count)], zu_s.at[n], zu_r.at[n], zdev(1))

    def zdn(n, count):
        return group(zsend.at[n, pl.ds(0, count)], zrecv.at[n, pl.ds(0, count)], zd_s.at[n], zd_r.at[n], zdev(1))

    def xdn(n, count, d):
        kind, half = CHUNKS[n]
        return group(xback.at[kind, pl.ds(0, count), half_rows(half)], before.at[kind, pl.ds(0, count), half_rows(half)],
                     xd_s.at[n], xd_r.at[n, d - 1], xdev(1))

    intra(0)
    for n in LATE_FIRST:
        kind, half = CHUNKS[n]
        xup(n).wait_recv()
        total = xrecv[kind, 0, half_rows(half), :]
        for i in range(1, X):
            total = total + xrecv[kind, i, half_rows(half), :]
        tbuf[kind, half_rows(half), :] = total
        if n == LATE_FIRST[0] and rounds:
            ring_wait(len(rounds) - 1)
        for d in zorder:
            to = (z + d) % nz

            @pl.when(owns(n, to))
            def _(n=n, kind=kind, d=d, to=to):
                pltpu.make_async_remote_copy(
                    tbuf.at[kind, owned(n, to)], zrecv.at[n, z], zu_s.at[n], arrival(n),
                    device_id=zdev(d), device_id_type=MESH).start()

    def give(n, to):
        kind = CHUNKS[n][0]

        @pl.when(z != to)
        def _():
            pltpu.make_async_remote_copy(
                zsend.at[n, to], zpre.at[kind, owned(n, z)], zd_s.at[n], zd_r.at[n],
                device_id=(to * X + x, seq), device_id_type=MESH).start()

        @pl.when(z == to)
        def _():
            zpre[kind, owned(n, z), :] = zsend[n, to]

    def arrived(n, sem, count):
        group(zsend.at[n, pl.ds(0, count)], zrecv.at[n, pl.ds(0, count)], zd_s.at[n], sem, zdev(1)).wait_recv()

    def scan_early(n):
        zrecv[n, z] = tbuf[0, owned(n, z), :]
        run = jnp.zeros((rows, DH), F32)
        for i in range(early + 1):
            zsend[n, i] = run
            give(n, i)
            if i < early:
                @pl.when(z != i)
                def _(i=i):
                    arrived(n, zk_r.at[n, i], 1)

                run = run + zrecv[n, i]

    def scan_late(n):
        @pl.when(z < early)
        def _():
            arrived(n, zk_r.at[n, early], nz - early)

        @pl.when(z >= early)
        def _():
            arrived(n, zk_r.at[n, early], nz - early - 1)

        run = zsend[n, early]
        for i in range(early, nz - 1):
            run = run + zrecv[n, i]
            zsend[n, i + 1] = run
        for i in range(early + 1, nz):
            give(n, i)

    def scan_back(n):
        zrecv[n, z] = tbuf[1, owned(n, z), :]
        arrived(n, zu_r.at[n], nz - 1)
        run = jnp.zeros((rows, DH), F32)
        for i in range(nz - 1, -1, -1):
            zsend[n, i] = run
            run = run + zrecv[n, i]
        for i in range(nz):
            give(n, i)

    intra(1)
    for scan, kind in ((scan_early, 0), (scan_back, 1), (scan_late, 0)):
        for half in range(HALVES):
            n = kind * HALVES + half

            @pl.when(owns(n, z))
            def _(scan=scan, n=n):
                scan(n)

    intra(2)
    for n, (kind, half) in enumerate(CHUNKS):
        @pl.when(owns(n, z))
        def _(n=n):
            zdn(n, owners - 1).wait_recv()

        @pl.when(jnp.logical_not(owns(n, z)))
        def _(n=n):
            zdn(n, owners).wait_recv()

        run = zpre[kind, half_rows(half), :]
        for i in (range(X) if kind == 0 else range(X - 1, -1, -1)):
            xback[kind, i, half_rows(half), :] = run
            run = run + xrecv[kind, i, half_rows(half), :]
        for d in (2, 1, 3):
            pltpu.make_async_remote_copy(
                xback.at[kind, (x + d) % X, half_rows(half)], before.at[kind, X - d, half_rows(half)],
                xd_s.at[n], xd_r.at[n, d - 1], device_id=xdev(d), device_id_type=MESH).start()
        before[kind, 0, half_rows(half), :] = xback[kind, x, half_rows(half), :]

    intra(3)
    for kind in range(2):
        for s in (0, 1, 3, 2):
            if s:
                for half in range(HALVES):
                    xdn(kind * HALVES + half, 1, X - s).wait_recv()
            for blk in range(nb):
                r = pl.ds(blk * BLOCK, BLOCK)
                low = (before[kind, s] + cum[kind, s, blk]).astype(BF16)
                if kind == 0:
                    first, second = dot(qs[r, cols(s)], low, 1, 0), dot(gs[r, cols(s)], low, 1, 1)
                else:
                    first, second = dot(vs[r, cols(s)], low, 1, 1), dot(ks[r, cols(s)], low, 1, 0)
                outs[2 * kind][r, cols(s)] = (part[2 * kind, s, r, :] + first).astype(BF16)
                outs[2 * kind + 1][r, cols(s)] = (part[2 * kind + 1, s, r, :] + second).astype(BF16)

    for n in range(len(CHUNKS)):
        xup(n).wait_send()

        @pl.when(owns(n, z))
        def _(n=n):
            zup(n, owners - 1).wait_send()
            zdn(n, nz - 1).wait_send()

        @pl.when(jnp.logical_not(owns(n, z)))
        def _(n=n):
            zup(n, owners).wait_send()

        xdn(n, X - 1, 1).wait_send()


def write_out(*refs):
    sem = refs[8]
    copies = [pltpu.make_async_copy(refs[i], refs[4 + i], sem.at[i]) for i in range(4)]
    for cp in copies:
        cp.start()
    for cp in copies:
        cp.wait()


def body(nz, queries, keys, values, out_grad):
    count, width = queries.shape
    nb = count // BLOCK
    assert width == X * DH
    assert nz % 3 == 0 and HALF * 3 % (2 * nz) == 0
    rows = HALF * 3 // (2 * nz)
    nc = len(CHUNKS)
    hbm = pl.BlockSpec(memory_space=pltpu.HBM)
    vmem = pl.BlockSpec(memory_space=pltpu.VMEM)
    vm = pltpu.VMEM
    dma = pltpu.SemaphoreType.DMA
    shape = jax.ShapeDtypeStruct((count, width), BF16)
    outs = pl.pallas_call(
        functools.partial(kernel, nz, nb),
        out_shape=(pltpu.VMEM((count, width), BF16),) * 4,
        in_specs=[hbm] * 4,
        out_specs=(vmem,) * 4,
        scratch_shapes=[
            vm((count, width), BF16),
            vm((count, width), BF16),
            vm((count, width), BF16),
            vm((count, width), BF16),
            vm((2, X, nb, DH, DH), F32),
            vm((4, X, count, DH), F32),
            vm((2, X - 1, DH, DH), F32),
            vm((2, X, DH, DH), F32),
            vm((2, DH, DH), F32),
            vm((nc, nz, rows, DH), F32),
            vm((nc, nz, rows, DH), F32),
            vm((2, DH, DH), F32),
            vm((2, X, DH, DH), F32),
            vm((2, X, DH, DH), F32),
            dma((2,)), dma((2, X)),
            pltpu.SemaphoreType.REGULAR((max(1, len(rounds_of(nz))),)),
            dma((nc,)), dma((nc,)),
            dma((nc,)), dma((nc,)), dma((HALVES, nz // 3 + 1)),
            dma((nc,)), dma((nc,)),
            dma((nc,)), dma((nc, X - 1)),
        ],
        compiler_params=pltpu.CompilerParams(
            collective_id=0, has_side_effects=True, vmem_limit_bytes=32 * 1024 * 1024),
    )(*(pltpu.with_memory_space_constraint(a, pltpu.HBM) for a in (queries, keys, values, out_grad)))
    return pl.pallas_call(
        write_out,
        out_shape=(shape,) * 4,
        in_specs=[vmem] * 4,
        out_specs=(hbm,) * 4,
        scratch_shapes=[dma((4,))],
    )(*(pltpu.with_memory_space_constraint(a, pltpu.VMEM) for a in outs))


def solution(mesh):
    nz = mesh.shape["ctx"] // X
    spec = P("ctx", "seq")
    return jax.shard_map(
        functools.partial(body, nz), mesh=mesh, in_specs=(spec,) * 4, out_specs=(spec,) * 4, check_vma=False)
```

```python
import functools

import jax
import jax.numpy as jnp
from jax import lax
from jax.experimental import pallas as pl
from jax.experimental.pallas import tpu as pltpu
from jax.sharding import PartitionSpec as P

DH = 128
BLOCK = 128
X = 4
HALVES = 2
HALF = DH // HALVES
CHUNKS = tuple((kind, half) for kind in range(2) for half in range(HALVES))
LATE_FIRST = tuple(sorted(range(len(CHUNKS)), key=lambda n: -CHUNKS[n][0]))
MESH = pl.DeviceIdType.MESH
F32 = jnp.float32
BF16 = jnp.bfloat16


def dot(a, b, ca, cb):
    return lax.dot_general(a, b, (((ca,), (cb,)), ((), ())), preferred_element_type=F32)


def rounds_of(nz):
    known, dists = 1, []
    while known < nz // 2:
        step = min(known, nz // 2 - known)
        dists.append(step)
        known += step
    return dists


def kernel(
    nz, nb, q_hbm, k_hbm, v_hbm, g_hbm, *refs,
):
    outs = refs[:4]
    (qs, ks, vs, gs, cum, part, xsend, xrecv, tbuf, zrecv, zsend, zpre, xback, before,
     in_sem, qg_sem, ring_sem, xu_s, xu_r, zu_s, zu_r, zk_r, zd_s, zd_r, xd_s, xd_r) = refs[4:]
    owners = 2 * nz // 3
    early = nz // 3
    rows = HALF // owners
    c = lax.axis_index("ctx")
    seq = lax.axis_index("seq")
    z = c // X
    x = c % X

    def xdev(d):
        return (z * X + (x + d) % X, seq)

    def zdev(d):
        return (((z + d) % nz) * X + x, seq)

    def both(d):
        return sorted({d, nz - d})

    def owns(n, at):
        return at % 3 != (2, 0, 1, 2)[n % 4]

    def owned(n, at):
        place = (at % 3, at % 3 - 1, (at % 3) // 2, at % 3)[n % 4]
        return pl.ds(pl.multiple_of((n % HALVES) * HALF + ((at // 3) * 2 + place) * rows, 8), rows)

    def arrival(n):
        return zk_r.at[n, jnp.minimum(z, early)] if CHUNKS[n][0] == 0 else zu_r.at[n]

    def half_rows(half):
        return pl.ds(half * HALF, HALF)

    zorder = sorted(range(1, nz), key=lambda d: -min(d, nz - d))
    rounds = rounds_of(nz)

    def cols(s):
        return pl.ds(pl.multiple_of(((x + s) % X) * DH, DH), DH)

    slots = (2, 1, 3, 0)
    loads = {}

    def load(i, hbm, buf):
        cp = pltpu.make_async_copy(hbm, buf, in_sem.at[i])
        cp.start()
        loads[i] = cp

    def load_head(s):
        for i, hbm, buf in ((0, q_hbm, qs), (1, g_hbm, gs)):
            cp = pltpu.make_async_copy(hbm.at[:, cols(s)], buf.at[:, cols(s)], qg_sem.at[i, s])
            cp.start()
            loads[i, s] = cp

    load_head(slots[0])
    barrier = pltpu.get_barrier_semaphore()
    for d in (2, 1, 3):
        pl.semaphore_signal(barrier, inc=1, device_id=xdev(d), device_id_type=MESH)
    for d in both(1):
        pl.semaphore_signal(barrier, inc=1, device_id=zdev(d), device_id_type=MESH)
    for s in slots[1:]:
        load_head(s)
    load(0, k_hbm, ks)
    load(1, v_hbm, vs)

    def ring_signal(i):
        for d in both(rounds[i]):
            pl.semaphore_signal(ring_sem.at[i], inc=1, device_id=zdev(d), device_id_type=MESH)

    def ring_wait(i):
        pl.semaphore_wait(ring_sem.at[i], len(both(rounds[i])))

    def local_state(kind, s):
        a, b = ((ks, vs), (qs, gs))[kind]
        run = jnp.zeros((DH, DH), F32)
        for blk in (range(nb) if kind == 0 else range(nb - 1, -1, -1)):
            cum[kind, s, blk] = run
            r = pl.ds(blk * BLOCK, BLOCK)
            run = run + dot(a[r, cols(s)], b[r, cols(s)], 0, 0)
        return run

    def send_state(kind, s, half):
        n = kind * HALVES + half
        pltpu.make_async_remote_copy(
            xsend.at[kind, s - 1, half_rows(half)], xrecv.at[kind, x, half_rows(half)], xu_s.at[n], xu_r.at[n],
            device_id=xdev(s), device_id_type=MESH).start()

    for kind in (1, 0):
        if kind == 0:
            loads[0].wait()
            loads[1].wait()
        for s in slots:
            if kind == 1:
                loads[0, s].wait()
                loads[1, s].wait()
            total = local_state(kind, s)
            if s == 0:
                xrecv[kind, x] = total
            else:
                xsend[kind, s - 1] = total
                if kind == 1 and s == slots[0]:
                    pl.semaphore_wait(barrier, X - 1 + len(both(1)))
                send_state(kind, s, 0)
        for half in range(1, HALVES):
            for s in slots[:-1]:
                send_state(kind, s, half)
        if kind == 1 and rounds:
            ring_signal(0)
    for i in range(1, len(rounds)):
        ring_wait(i - 1)
        ring_signal(i)

    tri = (lax.broadcasted_iota(jnp.int32, (BLOCK, BLOCK), 1)
           <= lax.broadcasted_iota(jnp.int32, (BLOCK, BLOCK), 0))

    def intra(s):
        for blk in range(nb):
            r = pl.ds(blk * BLOCK, BLOCK)
            q, k, v, g = qs[r, cols(s)], ks[r, cols(s)], vs[r, cols(s)], gs[r, cols(s)]
            attn = jnp.where(tri, dot(q, k, 1, 1), 0.0).astype(BF16)
            grads = jnp.where(tri, dot(g, v, 1, 1), 0.0).astype(BF16)
            part[0, s, r, :] = dot(attn, v, 1, 0)
            part[1, s, r, :] = dot(grads, k, 1, 0)
            part[2, s, r, :] = dot(grads, q, 0, 0)
            part[3, s, r, :] = dot(attn, g, 0, 0)

    def group(src, dst, send, recv, dev):
        return pltpu.make_async_remote_copy(src, dst, send, recv, device_id=dev, device_id_type=MESH)

    def xup(n):
        kind, half = CHUNKS[n]
        return group(xsend.at[kind, pl.ds(0, X - 1), half_rows(half)], xrecv.at[kind, pl.ds(0, X - 1), half_rows(half)],
                     xu_s.at[n], xu_r.at[n], xdev(1))

    def zup(n, count):
        return group(zsend.at[n, pl.ds(0, count)], zrecv.at[n, pl.ds(0, count)], zu_s.at[n], zu_r.at[n], zdev(1))

    def zdn(n, count):
        return group(zsend.at[n, pl.ds(0, count)], zrecv.at[n, pl.ds(0, count)], zd_s.at[n], zd_r.at[n], zdev(1))

    def xdn(n, count, d):
        kind, half = CHUNKS[n]
        return group(xback.at[kind, pl.ds(0, count), half_rows(half)], before.at[kind, pl.ds(0, count), half_rows(half)],
                     xd_s.at[n], xd_r.at[n, d - 1], xdev(1))

    intra(0)
    for n in LATE_FIRST:
        kind, half = CHUNKS[n]
        xup(n).wait_recv()
        total = xrecv[kind, 0, half_rows(half), :]
        for i in range(1, X):
            total = total + xrecv[kind, i, half_rows(half), :]
        tbuf[kind, half_rows(half), :] = total
        if n == LATE_FIRST[0] and rounds:
            ring_wait(len(rounds) - 1)
        for d in zorder:
            to = (z + d) % nz

            @pl.when(owns(n, to))
            def _(n=n, kind=kind, d=d, to=to):
                pltpu.make_async_remote_copy(
                    tbuf.at[kind, owned(n, to)], zrecv.at[n, z], zu_s.at[n], arrival(n),
                    device_id=zdev(d), device_id_type=MESH).start()

    def give(n, to):
        kind = CHUNKS[n][0]

        @pl.when(z != to)
        def _():
            pltpu.make_async_remote_copy(
                zsend.at[n, to], zpre.at[kind, owned(n, z)], zd_s.at[n], zd_r.at[n],
                device_id=(to * X + x, seq), device_id_type=MESH).start()

        @pl.when(z == to)
        def _():
            zpre[kind, owned(n, z), :] = zsend[n, to]

    def arrived(n, sem, count):
        group(zsend.at[n, pl.ds(0, count)], zrecv.at[n, pl.ds(0, count)], zd_s.at[n], sem, zdev(1)).wait_recv()

    def scan_early(n):
        zrecv[n, z] = tbuf[0, owned(n, z), :]
        run = jnp.zeros((rows, DH), F32)
        for i in range(early + 1):
            zsend[n, i] = run
            give(n, i)
            if i < early:
                @pl.when(z != i)
                def _(i=i):
                    arrived(n, zk_r.at[n, i], 1)

                run = run + zrecv[n, i]

    def scan_late(n):
        @pl.when(z < early)
        def _():
            arrived(n, zk_r.at[n, early], nz - early)

        @pl.when(z >= early)
        def _():
            arrived(n, zk_r.at[n, early], nz - early - 1)

        run = zsend[n, early]
        for i in range(early, nz - 1):
            run = run + zrecv[n, i]
            zsend[n, i + 1] = run
        for i in range(early + 1, nz):
            give(n, i)

    def scan_back(n):
        zrecv[n, z] = tbuf[1, owned(n, z), :]
        arrived(n, zu_r.at[n], nz - 1)
        run = jnp.zeros((rows, DH), F32)
        for i in range(nz - 1, -1, -1):
            zsend[n, i] = run
            run = run + zrecv[n, i]
        for i in range(nz):
            give(n, i)

    intra(1)
    for scan, kind in ((scan_early, 0), (scan_back, 1), (scan_late, 0)):
        for half in range(HALVES):
            n = kind * HALVES + half

            @pl.when(owns(n, z))
            def _(scan=scan, n=n):
                scan(n)

    intra(2)
    for n, (kind, half) in enumerate(CHUNKS):
        @pl.when(owns(n, z))
        def _(n=n):
            zdn(n, owners - 1).wait_recv()

        @pl.when(jnp.logical_not(owns(n, z)))
        def _(n=n):
            zdn(n, owners).wait_recv()

        run = zpre[kind, half_rows(half), :]
        for i in (range(X) if kind == 0 else range(X - 1, -1, -1)):
            xback[kind, i, half_rows(half), :] = run
            run = run + xrecv[kind, i, half_rows(half), :]
        for d in (2, 1, 3):
            pltpu.make_async_remote_copy(
                xback.at[kind, (x + d) % X, half_rows(half)], before.at[kind, X - d, half_rows(half)],
                xd_s.at[n], xd_r.at[n, d - 1], device_id=xdev(d), device_id_type=MESH).start()
        before[kind, 0, half_rows(half), :] = xback[kind, x, half_rows(half), :]

    intra(3)
    for kind in range(2):
        for s in (0, 1, 3, 2):
            if s:
                for half in range(HALVES):
                    xdn(kind * HALVES + half, 1, X - s).wait_recv()
            for blk in range(nb):
                r = pl.ds(blk * BLOCK, BLOCK)
                low = (before[kind, s] + cum[kind, s, blk]).astype(BF16)
                if kind == 0:
                    first, second = dot(qs[r, cols(s)], low, 1, 0), dot(gs[r, cols(s)], low, 1, 1)
                else:
                    first, second = dot(vs[r, cols(s)], low, 1, 1), dot(ks[r, cols(s)], low, 1, 0)
                outs[2 * kind][r, cols(s)] = (part[2 * kind, s, r, :] + first).astype(BF16)
                outs[2 * kind + 1][r, cols(s)] = (part[2 * kind + 1, s, r, :] + second).astype(BF16)

    for n in range(len(CHUNKS)):
        xup(n).wait_send()

        @pl.when(owns(n, z))
        def _(n=n):
            zup(n, owners - 1).wait_send()
            zdn(n, nz - 1).wait_send()

        @pl.when(jnp.logical_not(owns(n, z)))
        def _(n=n):
            zup(n, owners).wait_send()

        xdn(n, X - 1, 1).wait_send()


def write_out(*refs):
    sem = refs[8]
    half = refs[0].shape[0] // 2
    copies = [
        pltpu.make_async_copy(refs[i].at[pl.ds(j * half, half)], refs[4 + i].at[pl.ds(j * half, half)], sem.at[i, j])
        for i in range(4) for j in range(2)
    ]
    for cp in copies:
        cp.start()
    for cp in copies:
        cp.wait()


def body(nz, queries, keys, values, out_grad):
    count, width = queries.shape
    nb = count // BLOCK
    assert width == X * DH
    assert nz % 3 == 0 and HALF * 3 % (2 * nz) == 0
    rows = HALF * 3 // (2 * nz)
    nc = len(CHUNKS)
    hbm = pl.BlockSpec(memory_space=pltpu.HBM)
    vmem = pl.BlockSpec(memory_space=pltpu.VMEM)
    vm = pltpu.VMEM
    dma = pltpu.SemaphoreType.DMA
    shape = jax.ShapeDtypeStruct((count, width), BF16)
    outs = pl.pallas_call(
        functools.partial(kernel, nz, nb),
        out_shape=(pltpu.VMEM((count, width), BF16),) * 4,
        in_specs=[hbm] * 4,
        out_specs=(vmem,) * 4,
        scratch_shapes=[
            vm((count, width), BF16),
            vm((count, width), BF16),
            vm((count, width), BF16),
            vm((count, width), BF16),
            vm((2, X, nb, DH, DH), F32),
            vm((4, X, count, DH), F32),
            vm((2, X - 1, DH, DH), F32),
            vm((2, X, DH, DH), F32),
            vm((2, DH, DH), F32),
            vm((nc, nz, rows, DH), F32),
            vm((nc, nz, rows, DH), F32),
            vm((2, DH, DH), F32),
            vm((2, X, DH, DH), F32),
            vm((2, X, DH, DH), F32),
            dma((2,)), dma((2, X)),
            pltpu.SemaphoreType.REGULAR((max(1, len(rounds_of(nz))),)),
            dma((nc,)), dma((nc,)),
            dma((nc,)), dma((nc,)), dma((HALVES, nz // 3 + 1)),
            dma((nc,)), dma((nc,)),
            dma((nc,)), dma((nc, X - 1)),
        ],
        compiler_params=pltpu.CompilerParams(
            collective_id=0, has_side_effects=True, vmem_limit_bytes=32 * 1024 * 1024),
    )(*(pltpu.with_memory_space_constraint(a, pltpu.HBM) for a in (queries, keys, values, out_grad)))
    return pl.pallas_call(
        write_out,
        out_shape=(shape,) * 4,
        in_specs=[vmem] * 4,
        out_specs=(hbm,) * 4,
        scratch_shapes=[dma((4, 2))],
    )(*(pltpu.with_memory_space_constraint(a, pltpu.VMEM) for a in outs))


def solution(mesh):
    nz = mesh.shape["ctx"] // X
    spec = P("ctx", "seq")
    return jax.shard_map(
        functools.partial(body, nz), mesh=mesh, in_specs=(spec,) * 4, out_specs=(spec,) * 4, check_vma=False)
```
